32 devices in a mesh: tok: 8 (over z, x), head: 4 (over y, core).
Axes of the slice: x: 2, y: 2, z: 4, core: 2. Of those that a mesh axis runs over, the one named last changes fastest.
Arguments:
- queries: bfloat16 [8192, 4096], P(('tok', 'head')), may hold values from -6 to 6
- key_tokens: bfloat16 [8192, 4096], P(('tok', 'head')), may hold values from -6 to 6
- values: bfloat16 [8192, 4096], P(('tok', 'head')), may hold values from -6 to 6
- out_grad: bfloat16 [8192, 4096], P(('tok', 'head')), may hold values from -6 to 6
- learn_rates: float32 [8192, 16], P('tok', 'head'), may hold values from 0.2 to 2
- w_gate: bfloat16 [16, 256, 256], P('head'), may hold values from -0.375 to 0.375
- w_up: bfloat16 [16, 256, 256], P('head'), may hold values from -0.375 to 0.375
- w_down: bfloat16 [16, 256, 256], P('head'), may hold values from -0.375 to 0.375
Outputs:
- grad_queries: bfloat16 [8192, 4096], P(('tok', 'head'))
- grad_keys: bfloat16 [8192, 4096], P(('tok', 'head'))
- grad_values: bfloat16 [8192, 4096], P(('tok', 'head'))
The draws below stay inside these ranges and needn't reach their ends.
All inputs are finite; a program needn't handle non-finite values.
Results may differ from the reference program's by a relative error of at most 0.02.
Values may be sent and summed in bfloat16 or wider, within the bound.
No kernel may reach another device: no remote copies, remote signals or barrier semaphores. Data moves between devices by JAX's collectives and lax.ppermute only.
A program may use at most 128 MiB of HBM per device.

```python
import math
import jax
import jax.numpy as jnp

H = 16
DH = 256
D = 4096
TOKENS = 8192


def shard_levels(key, extent, pieces, low, top_value):
    def one(position, shards_of):
        draws = jax.random.uniform(jax.random.fold_in(jax.random.fold_in(key, 6), position), (shards_of,), jnp.float32, low / len(pieces), top_value / len(pieces))
        return jnp.repeat(jnp.exp(draws), extent[position] // shards_of).reshape((-1,) + (1,) * (len(extent) - position - 1))

    level = one(*pieces[0])
    for cut in pieces[1:]:
        level = level * one(*cut)
    return level


def noise(key, shape, scale, reach, split=(), held_as=jnp.bfloat16):
    loudness = shard_levels(key, shape, split, -0.22, 0.18) if split else 1.0
    values = jax.random.normal(key, shape, jnp.float32) * scale * loudness
    return jnp.minimum(jnp.maximum(values, -reach), reach).astype(held_as)


def setup_inputs(seed: int = 0) -> dict:
    seeds = jax.random.split(jax.random.key(seed), 9)
    queries = noise(seeds[0], (TOKENS, D), 1.0, 6.0, ((0, 32),))
    key_tokens = noise(seeds[1], (TOKENS, D), 1.0, 6.0, ((0, 32),))
    values = noise(seeds[2], (TOKENS, D), 1.0, 6.0, ((0, 32),))
    out_grad = noise(seeds[3], (TOKENS, D), 1.0, 6.0, ((0, 32),))
    learn_rates = jnp.clip(jnp.exp(math.log(2.0) - 2.3025851 * jax.random.uniform(seeds[4], (TOKENS, H), jnp.float32) ** shard_levels(seeds[4], (TOKENS, H), ((0, 8), (1, 4)), -0.2, 0.2)), 0.2, 2.0)
    w_gate = noise(seeds[5], (H, DH, DH), DH ** -0.5, 0.375, ((0, 4),))
    w_up = noise(seeds[6], (H, DH, DH), DH ** -0.5, 0.375, ((0, 4),))
    w_down = noise(seeds[7], (H, DH, DH), DH ** -0.5, 0.375, ((0, 4),))
    return {"queries": queries, "key_tokens": key_tokens, "values": values, "out_grad": out_grad, "learn_rates": learn_rates, "w_gate": w_gate, "w_up": w_up, "w_down": w_down}


def silu_slope(pre_act):
    sigmoid_val = jax.nn.sigmoid(pre_act)
    return sigmoid_val * (1.0 + pre_act * (1.0 - sigmoid_val))

def silu_curve(pre_act):
    sigmoid_val = jax.nn.sigmoid(pre_act)
    return sigmoid_val * (1.0 - sigmoid_val) * (2.0 + pre_act * (1.0 - 2.0 * sigmoid_val))

def key_forward(key_rows, scaled, gate_mat, up_mat, down_mat):
    gate_pre = jnp.dot(key_rows, gate_mat, preferred_element_type=jnp.float32)
    up_pre = jnp.dot(key_rows, up_mat, preferred_element_type=jnp.float32)
    gate_act = jax.nn.silu(gate_pre)
    hidden = (gate_act * up_pre).astype(jnp.bfloat16)
    key_dhid = jnp.dot(scaled, down_mat.T, preferred_element_type=jnp.float32)
    grad_gate = (key_dhid * up_pre * silu_slope(gate_pre)).astype(jnp.bfloat16)
    grad_upper = (key_dhid * gate_act).astype(jnp.bfloat16)
    delta_gate = jnp.dot(key_rows.T, grad_gate, preferred_element_type=jnp.float32)
    delta_up = jnp.dot(key_rows.T, grad_upper, preferred_element_type=jnp.float32)
    delta_down = jnp.dot(hidden.T, scaled, preferred_element_type=jnp.float32)
    stored = (gate_pre, up_pre, hidden, key_dhid, grad_gate, grad_upper)
    return ((delta_gate, delta_up, delta_down), stored)

def query_side(query_rows, out_rows, fresh_gate, fresh_up, fresh_down):
    gate_pre = jnp.dot(query_rows, fresh_gate, preferred_element_type=jnp.float32)
    up_pre = jnp.dot(query_rows, fresh_up, preferred_element_type=jnp.float32)
    gate_act = jax.nn.silu(gate_pre)
    hidden = (gate_act * up_pre).astype(jnp.bfloat16)
    query_dhid = jnp.dot(out_rows, fresh_down.T, preferred_element_type=jnp.float32)
    grad_gate = (query_dhid * up_pre * silu_slope(gate_pre)).astype(jnp.bfloat16)
    grad_upper = (query_dhid * gate_act).astype(jnp.bfloat16)
    query_grad = jnp.dot(grad_gate, fresh_gate.T, preferred_element_type=jnp.float32)
    query_grad = query_grad + jnp.dot(grad_upper, fresh_up.T, preferred_element_type=jnp.float32)
    sum_gate = jnp.dot(query_rows.T, grad_gate, preferred_element_type=jnp.float32)
    sum_up = jnp.dot(query_rows.T, grad_upper, preferred_element_type=jnp.float32)
    sum_down = jnp.dot(hidden.T, out_rows, preferred_element_type=jnp.float32)
    return (query_grad.astype(jnp.bfloat16), (sum_gate, sum_up, sum_down))

def key_back(key_rows, scaled, rate_col, gate_mat, up_mat, down_mat, stored, adj_gate, adj_up, adj_down):
    gate_pre, up_pre, hidden, key_dhid, grad_gate, grad_upper = stored
    back_dgate = jnp.dot(key_rows, adj_gate, preferred_element_type=jnp.float32)
    back_dup = jnp.dot(key_rows, adj_up, preferred_element_type=jnp.float32)
    back_hidden = jnp.dot(scaled, adj_down.T, preferred_element_type=jnp.float32)
    back_scaled = jnp.dot(hidden, adj_down, preferred_element_type=jnp.float32)
    gate_act = jax.nn.silu(gate_pre)
    gate_slope = silu_slope(gate_pre)
    back_dhid = (back_dgate * up_pre * gate_slope + back_dup * gate_act).astype(jnp.bfloat16)
    back_gate = (back_dgate * key_dhid * up_pre * silu_curve(gate_pre) + (back_dup * key_dhid + back_hidden * up_pre) * gate_slope).astype(jnp.bfloat16)
    back_upper = (back_dgate * key_dhid * gate_slope + back_hidden * gate_act).astype(jnp.bfloat16)
    key_grad = jnp.dot(grad_gate, adj_gate.T, preferred_element_type=jnp.float32)
    key_grad = key_grad + jnp.dot(grad_upper, adj_up.T, preferred_element_type=jnp.float32)
    key_grad = key_grad + jnp.dot(back_gate, gate_mat.T, preferred_element_type=jnp.float32)
    key_grad = key_grad + jnp.dot(back_upper, up_mat.T, preferred_element_type=jnp.float32)
    value_grad = rate_col[:, None] * (back_scaled + jnp.dot(back_dhid, down_mat, preferred_element_type=jnp.float32))
    return (key_grad.astype(jnp.bfloat16), value_grad.astype(jnp.bfloat16))

def reference(queries, key_tokens, values, out_grad, learn_rates, w_gate, w_up, w_down):
    update_scale = 1.0 / math.sqrt(DH * TOKENS)
    query_list = []
    key_list = []
    value_list = []
    for head_index in range(H):
        first = head_index * DH
        key_rows = key_tokens[:, first:first + DH]
        query_rows = queries[:, first:first + DH]
        out_rows = out_grad[:, first:first + DH]
        rate_col = learn_rates[:, head_index]
        scaled = (rate_col[:, None] * values[:, first:first + DH].astype(jnp.float32)).astype(jnp.bfloat16)
        deltas, stored = key_forward(key_rows, scaled, w_gate[head_index], w_up[head_index], w_down[head_index])
        fresh_gate = (w_gate[head_index].astype(jnp.float32) + update_scale * deltas[0]).astype(jnp.bfloat16)
        fresh_up = (w_up[head_index].astype(jnp.float32) + update_scale * deltas[1]).astype(jnp.bfloat16)
        fresh_down = (w_down[head_index].astype(jnp.float32) + update_scale * deltas[2]).astype(jnp.bfloat16)
        query_grad, sums = query_side(query_rows, out_rows, fresh_gate, fresh_up, fresh_down)
        adj_gate = (update_scale * sums[0]).astype(jnp.bfloat16)
        adj_up = (update_scale * sums[1]).astype(jnp.bfloat16)
        adj_down = (update_scale * sums[2]).astype(jnp.bfloat16)
        key_grad, value_grad = key_back(key_rows, scaled, rate_col, w_gate[head_index], w_up[head_index], w_down[head_index], stored, adj_gate, adj_up, adj_down)
        query_list.append(query_grad)
        key_list.append(key_grad)
        value_list.append(value_grad)
    return (jnp.concatenate(query_list, axis=1), jnp.concatenate(key_list, axis=1), jnp.concatenate(value_list, axis=1))
```

```python
import functools
import math

import jax
import jax.numpy as jnp
from jax import lax
from jax.experimental import pallas as pl
from jax.experimental.pallas import tpu as pltpu
from jax.sharding import Mesh, PartitionSpec as P

F32 = jnp.float32
BF16 = jnp.bfloat16


def mm(a, b):
    return lax.dot_general(a, b, (((1,), (0,)), ((), ())), preferred_element_type=F32)


def mm_nt(a, b):
    return lax.dot_general(a, b, (((1,), (1,)), ((), ())), preferred_element_type=F32)


def mm_tn(a, b):
    return lax.dot_general(a, b, (((0,), (0,)), ((), ())), preferred_element_type=F32)


def wide(rate, columns):
    return jnp.concatenate([rate] * (columns // rate.shape[1]), axis=1)


def rows_of(ref, which):
    block = ref[:, which]
    return block.reshape(block.shape[0] * block.shape[1], block.shape[2])


def put_rows(ref, which, value):
    ref[:, which] = value.reshape(ref.shape[0], ref.shape[2], ref.shape[3])


def key_kernel(s_ref, kv_ref, rate_ref, wg_ref, wu_ref, wd_ref, part_ref, sent_ref):
    step = pl.program_id(0)
    width = kv_ref.shape[-1]
    k = rows_of(kv_ref, 0)
    scaled = (wide(rate_ref[...], width) * rows_of(kv_ref, 1).astype(F32)).astype(BF16)
    gate = mm(k, wg_ref[0])
    up = mm(k, wu_ref[0])
    dhid = mm_nt(scaled, wd_ref[0])
    sig = jax.nn.sigmoid(gate)
    act = gate * sig
    hidden = (act * up).astype(BF16)
    dgate = (dhid * up * (sig * (1.0 + gate * (1.0 - sig)))).astype(BF16)
    dup = (dhid * act).astype(BF16)

    @pl.when(step == 0)
    def _():
        part_ref[...] = jnp.zeros_like(part_ref)

    part_ref[0] += mm_tn(k, dgate)
    part_ref[1] += mm_tn(k, dup)
    part_ref[2] += mm_tn(hidden, scaled)

    @pl.when(step == pl.num_programs(0) - 1)
    def _():
        sent_ref[...] = part_ref[...].astype(BF16)


def query_kernel(
    scale, s_ref, qo_ref, wg_ref, wu_ref, wd_ref, own_ref, other_ref, gq_ref, part_ref, sent_ref, fresh
):
    step = pl.program_id(0)

    @pl.when(step == 0)
    def _():
        part_ref[...] = jnp.zeros_like(part_ref)
        for i, w_ref in enumerate((wg_ref, wu_ref, wd_ref)):
            total = own_ref[i] + other_ref[i].astype(F32)
            fresh[i] = (w_ref[0].astype(F32) + scale * total).astype(BF16)

    q = rows_of(qo_ref, 0)
    o = rows_of(qo_ref, 1)
    gate = mm(q, fresh[0])
    up = mm(q, fresh[1])
    dhid = mm_nt(o, fresh[2])
    sig = jax.nn.sigmoid(gate)
    act = gate * sig
    hidden = (act * up).astype(BF16)
    dgate = (dhid * up * (sig * (1.0 + gate * (1.0 - sig)))).astype(BF16)
    dup = (dhid * act).astype(BF16)
    grad = mm_nt(dgate, fresh[0]) + mm_nt(dup, fresh[1])
    gq_ref[...] = grad.astype(BF16).reshape(gq_ref.shape)
    part_ref[0] += mm_tn(q, dgate)
    part_ref[1] += mm_tn(q, dup)
    part_ref[2] += mm_tn(hidden, o)

    @pl.when(step == pl.num_programs(0) - 1)
    def _():
        sent_ref[...] = part_ref[...].astype(BF16)


def back_kernel(
    scale, s_ref, kv_ref, rate_ref, wg_ref, wu_ref, wd_ref, own_ref, other_ref, gkv_ref, adj
):
    step = pl.program_id(0)

    @pl.when(step == 0)
    def _():
        adj[...] = (scale * (own_ref[...] + other_ref[...].astype(F32))).astype(BF16)

    width = kv_ref.shape[-1]
    k = rows_of(kv_ref, 0)
    rate = wide(rate_ref[...], width)
    scaled = (rate * rows_of(kv_ref, 1).astype(F32)).astype(BF16)
    gate = mm(k, wg_ref[0])
    up = mm(k, wu_ref[0])
    dhid = mm_nt(scaled, wd_ref[0])
    sig = jax.nn.sigmoid(gate)
    act = gate * sig
    rest = 1.0 - sig
    slope = sig * (1.0 + gate * rest)
    curve = sig * rest * (2.0 + gate * (1.0 - 2.0 * sig))
    hidden = (act * up).astype(BF16)
    dgate = (dhid * up * slope).astype(BF16)
    dup = (dhid * act).astype(BF16)
    back_dgate = mm(k, adj[0])
    back_dup = mm(k, adj[1])
    back_hidden = mm_nt(scaled, adj[2])
    back_scaled = mm(hidden, adj[2])
    back_dhid = (back_dgate * up * slope + back_dup * act).astype(BF16)
    back_gate = (
        back_dgate * dhid * up * curve + (back_dup * dhid + back_hidden * up) * slope
    ).astype(BF16)
    back_upper = (back_dgate * dhid * slope + back_hidden * act).astype(BF16)
    grad_k = mm_nt(dgate, adj[0]) + mm_nt(dup, adj[1])
    grad_k = grad_k + mm_nt(back_gate, wg_ref[0]) + mm_nt(back_upper, wu_ref[0])
    grad_v = rate * (back_scaled + mm(back_dhid, wd_ref[0]))
    put_rows(gkv_ref, 0, grad_k.astype(BF16))
    put_rows(gkv_ref, 1, grad_v.astype(BF16))


def blocks_per_step(pieces, rows, most):
    best = 1
    for n in range(1, pieces + 1):
        if pieces % n == 0 and n * rows <= most:
            best = n
    return best


def body(n_t, n_s, n_head, queries, key_tokens, values, out_grad, learn_rates, w_gate, w_up, w_down):
    rows, model = queries.shape
    heads = n_head * n_s
    dim = model // heads
    pieces = heads
    spread = ("head", "s")
    place = lax.axis_index("s").astype(jnp.int32).reshape(1)
    scale = 1.0 / math.sqrt(dim * rows * pieces * n_t)

    def by_head(x):
        return x.reshape(rows, heads, dim).transpose(1, 0, 2)

    def exchange(x):
        return lax.all_to_all(x, spread, split_axis=0, concat_axis=0, tiled=True)

    def pair(own, sent):
        if n_t == 1:
            return own, jnp.zeros_like(sent)
        if n_t == 2:
            return own, lax.ppermute(sent, "t", [(0, 1), (1, 0)])
        return jnp.zeros_like(own), lax.psum(sent, "t")

    kv = exchange(jnp.stack([by_head(key_tokens), by_head(values)], axis=1))
    rate = lax.all_to_all(learn_rates.T, "s", split_axis=0, concat_axis=0, tiled=True)
    rate = rate.reshape(n_s, n_head, rows).transpose(1, 0, 2).reshape(pieces * rows, 1)
    rate = jnp.broadcast_to(rate, (pieces * rows, min(128, dim)))
    qo = exchange(jnp.stack([by_head(queries), by_head(out_grad)], axis=1))

    per = blocks_per_step(pieces, rows, 1024)
    grid = (pieces // per,)
    two_spec = pl.BlockSpec((per, 2, rows, dim), lambda i, s: (i, 0, 0, 0))
    one_spec = pl.BlockSpec((per, rows, dim), lambda i, s: (i, 0, 0))
    rate_spec = pl.BlockSpec((per * rows, rate.shape[1]), lambda i, s: (i, 0))
    w_spec = pl.BlockSpec((1, dim, dim), lambda i, s: (s[0], 0, 0))
    sum_spec = pl.BlockSpec((3, dim, dim), lambda i, s: (0, 0, 0))
    sum_shapes = [
        jax.ShapeDtypeStruct((3, dim, dim), F32),
        jax.ShapeDtypeStruct((3, dim, dim), BF16),
    ]
    params = pltpu.CompilerParams(
        dimension_semantics=("arbitrary",), vmem_limit_bytes=56 * 1024 * 1024
    )

    part, sent = pl.pallas_call(
        key_kernel,
        out_shape=sum_shapes,
        grid_spec=pltpu.PrefetchScalarGridSpec(
            num_scalar_prefetch=1,
            grid=grid,
            in_specs=[two_spec, rate_spec, w_spec, w_spec, w_spec],
            out_specs=[sum_spec, sum_spec],
        ),
        compiler_params=params,
        name="key_forward",
    )(place, kv, rate, w_gate, w_up, w_down)
    own, other = pair(part, sent)
    grad_q, part, sent = pl.pallas_call(
        functools.partial(query_kernel, scale),
        out_shape=[jax.ShapeDtypeStruct((pieces, rows, dim), BF16)] + sum_shapes,
        grid_spec=pltpu.PrefetchScalarGridSpec(
            num_scalar_prefetch=1,
            grid=grid,
            in_specs=[two_spec, w_spec, w_spec, w_spec, sum_spec, sum_spec],
            out_specs=[one_spec, sum_spec, sum_spec],
            scratch_shapes=[pltpu.VMEM((3, dim, dim), BF16)],
        ),
        compiler_params=params,
        name="query_side",
    )(place, qo, w_gate, w_up, w_down, own, other)
    own, other = pair(part, sent)
    grad_q = exchange(grad_q)
    grad_kv = pl.pallas_call(
        functools.partial(back_kernel, scale),
        out_shape=jax.ShapeDtypeStruct((pieces, 2, rows, dim), BF16),
        grid_spec=pltpu.PrefetchScalarGridSpec(
            num_scalar_prefetch=1,
            grid=grid,
            in_specs=[two_spec, rate_spec, w_spec, w_spec, w_spec, sum_spec, sum_spec],
            out_specs=two_spec,
            scratch_shapes=[pltpu.VMEM((3, dim, dim), BF16)],
        ),
        compiler_params=params,
        name="key_back",
    )(place, kv, rate, w_gate, w_up, w_down, own, other)
    grad_kv = exchange(grad_kv)

    def home(x):
        return x.transpose(1, 0, 2).reshape(rows, model)

    return home(grad_q), home(grad_kv[:, 0]), home(grad_kv[:, 1])


def solution(mesh):
    n_tok, n_head = mesh.shape["tok"], mesh.shape["head"]

    def run(queries, key_tokens, values, out_grad, learn_rates, w_gate, w_up, w_down):
        n_s = w_gate.shape[0] // n_head
        n_t = n_tok // n_s
        split = Mesh(mesh.devices.reshape(n_t, n_s, n_head), ("t", "s", "head"))
        tokens = P(("t", "s", "head"), None)
        weights = P("head", None, None)
        return jax.shard_map(
            functools.partial(body, n_t, n_s, n_head),
            mesh=split,
            in_specs=(tokens,) * 4 + (P(("t", "s"), "head"),) + (weights,) * 3,
            out_specs=(tokens,) * 3,
            check_vma=False,
        )(queries, key_tokens, values, out_grad, learn_rates, w_gate, w_up, w_down)

    return run
```

```python
import functools
import math

import jax
import jax.numpy as jnp
from jax import lax
from jax.experimental import pallas as pl
from jax.experimental.pallas import tpu as pltpu
from jax.sharding import Mesh, PartitionSpec as P


F32 = jnp.float32
BF16 = jnp.bfloat16


def mm(a, b):
    return lax.dot_general(a, b, (((1,), (0,)), ((), ())), preferred_element_type=F32)


def mm_nt(a, b):
    return lax.dot_general(a, b, (((1,), (1,)), ((), ())), preferred_element_type=F32)


def mm_tn(a, b):
    return lax.dot_general(a, b, (((0,), (0,)), ((), ())), preferred_element_type=F32)


def swap_out_kernel(first_ref, second_ref, out_ref):
    dim = out_ref.shape[-1]
    for h in range(out_ref.shape[0]):
        out_ref[h, 0] = first_ref[:, h * dim : (h + 1) * dim]
        out_ref[h, 1] = second_ref[:, h * dim : (h + 1) * dim]


def home_two_kernel(in_ref, first_ref, second_ref):
    dim = in_ref.shape[-1]
    for h in range(in_ref.shape[0]):
        first_ref[:, h * dim : (h + 1) * dim] = in_ref[h, 0]
        second_ref[:, h * dim : (h + 1) * dim] = in_ref[h, 1]


def home_one_kernel(in_ref, out_ref):
    dim = in_ref.shape[-1]
    for h in range(in_ref.shape[0]):
        out_ref[:, h * dim : (h + 1) * dim] = in_ref[h]


def spread_rates(s_ref, rates, n_s, per, dim):
    n_head = rates.shape[0] // n_s
    columns = []
    for j in range(per):
        piece = pl.program_id(0) * per + j
        back = lax.rem(s_ref[0] - lax.rem(piece, n_s) + n_s, n_s)
        row = rates[pl.ds(back * n_head + piece // n_s, 1), :]
        columns.append(jnp.broadcast_to(row, (128, row.shape[1])).T)
    tall = jnp.concatenate(columns, axis=0)
    return jnp.concatenate([tall] * (dim // 128), axis=1)


def pack_rates_kernel(*refs):
    n_head = refs[0].shape[0]
    for j, ref in enumerate(refs[:-1]):
        refs[-1][j * n_head : (j + 1) * n_head, :] = ref[...]


def rows_of(ref, which):
    block = ref[:, which]
    return block.reshape(block.shape[0] * block.shape[1], block.shape[2])


def put_rows(ref, which, value):
    ref[:, which] = value.reshape(ref.shape[0], ref.shape[2], ref.shape[3])


def key_kernel(n_s, s_ref, kv_ref, rate_ref, wg_ref, wu_ref, wd_ref, part_ref, sent_ref):
    step = pl.program_id(0)

    @pl.when(step == 0)
    def _():
        part_ref[...] = jnp.zeros_like(part_ref)

    rate = spread_rates(s_ref, rate_ref, n_s, kv_ref.shape[0], kv_ref.shape[-1])
    k = rows_of(kv_ref, 0)
    scaled = (rate * rows_of(kv_ref, 1).astype(F32)).astype(BF16)
    gate = mm(k, wg_ref[0])
    up = mm(k, wu_ref[0])
    dhid = mm_nt(scaled, wd_ref[0])
    sig = jax.nn.sigmoid(gate)
    act = gate * sig
    hidden = (act * up).astype(BF16)
    dgate = (dhid * up * (sig * (1.0 + gate * (1.0 - sig)))).astype(BF16)
    dup = (dhid * act).astype(BF16)
    part_ref[0] += mm_tn(k, dgate)
    part_ref[1] += mm_tn(k, dup)
    part_ref[2] += mm_tn(hidden, scaled)

    @pl.when(step == pl.num_programs(0) - 1)
    def _():
        sent_ref[...] = part_ref[...].astype(BF16)


def query_kernel(
    scale, s_ref, qo_ref, wg_ref, wu_ref, wd_ref, own_ref, other_ref, gq_ref, part_ref, sent_ref, fresh
):
    step = pl.program_id(0)

    @pl.when(step == 0)
    def _():
        part_ref[...] = jnp.zeros_like(part_ref)
        for i, w_ref in enumerate((wg_ref, wu_ref, wd_ref)):
            total = own_ref[i] + other_ref[i].astype(F32)
            fresh[i] = (w_ref[0].astype(F32) + scale * total).astype(BF16)

    q = rows_of(qo_ref, 0)
    o = rows_of(qo_ref, 1)
    gate = mm(q, fresh[0])
    up = mm(q, fresh[1])
    dhid = mm_nt(o, fresh[2])
    sig = jax.nn.sigmoid(gate)
    act = gate * sig
    hidden = (act * up).astype(BF16)
    dgate = (dhid * up * (sig * (1.0 + gate * (1.0 - sig)))).astype(BF16)
    dup = (dhid * act).astype(BF16)
    grad = mm_nt(dgate, fresh[0]) + mm_nt(dup, fresh[1])
    gq_ref[...] = grad.astype(BF16).reshape(gq_ref.shape)
    part_ref[0] += mm_tn(q, dgate)
    part_ref[1] += mm_tn(q, dup)
    part_ref[2] += mm_tn(hidden, o)

    @pl.when(step == pl.num_programs(0) - 1)
    def _():
        sent_ref[...] = part_ref[...].astype(BF16)


def back_kernel(
    scale, n_s, s_ref, kv_ref, rate_ref, wg_ref, wu_ref, wd_ref, own_ref, other_ref, gkv_ref, adj
):
    step = pl.program_id(0)

    @pl.when(step == 0)
    def _():
        adj[...] = (scale * (own_ref[...] + other_ref[...].astype(F32))).astype(BF16)

    rate = spread_rates(s_ref, rate_ref, n_s, kv_ref.shape[0], kv_ref.shape[-1])
    k = rows_of(kv_ref, 0)
    scaled = (rate * rows_of(kv_ref, 1).astype(F32)).astype(BF16)
    gate = mm(k, wg_ref[0])
    up = mm(k, wu_ref[0])
    dhid = mm_nt(scaled, wd_ref[0])
    sig = jax.nn.sigmoid(gate)
    act = gate * sig
    rest = 1.0 - sig
    slope = sig * (1.0 + gate * rest)
    curve = sig * rest * (2.0 + gate * (1.0 - 2.0 * sig))
    hidden = (act * up).astype(BF16)
    dgate = (dhid * up * slope).astype(BF16)
    dup = (dhid * act).astype(BF16)
    back_dgate = mm(k, adj[0])
    back_dup = mm(k, adj[1])
    back_hidden = mm_nt(scaled, adj[2])
    back_scaled = mm(hidden, adj[2])
    back_dhid = (back_dgate * up * slope + back_dup * act).astype(BF16)
    back_gate = (
        back_dgate * dhid * up * curve + (back_dup * dhid + back_hidden * up) * slope
    ).astype(BF16)
    back_upper = (back_dgate * dhid * slope + back_hidden * act).astype(BF16)
    grad_k = mm_nt(dgate, adj[0]) + mm_nt(dup, adj[1])
    grad_k = grad_k + mm_nt(back_gate, wg_ref[0]) + mm_nt(back_upper, wu_ref[0])
    grad_v = rate * (back_scaled + mm(back_dhid, wd_ref[0]))
    put_rows(gkv_ref, 0, grad_k.astype(BF16))
    put_rows(gkv_ref, 1, grad_v.astype(BF16))


def blocks_per_step(pieces, rows, most):
    best = 1
    for n in range(1, pieces + 1):
        if pieces % n == 0 and n * rows <= most:
            best = n
    return best


def body(n_t, n_s, n_head, queries, key_tokens, values, out_grad, learn_rates, w_gate, w_up, w_down):
    rows, model = queries.shape
    heads = n_head * n_s
    dim = model // heads
    pieces = heads
    spread = ("head", "s")
    place = lax.axis_index("s").astype(jnp.int32).reshape(1)
    scale = 1.0 / math.sqrt(dim * rows * pieces * n_t)

    block = min(rows, 128)
    copy_grid = (rows // block,)
    flat_spec = pl.BlockSpec((block, model), lambda i: (i, 0))
    pair_spec = pl.BlockSpec((heads, 2, block, dim), lambda i: (0, 0, i, 0))

    def by_head(first, second):
        return pl.pallas_call(
            swap_out_kernel,
            out_shape=jax.ShapeDtypeStruct((heads, 2, rows, dim), BF16),
            grid=copy_grid,
            in_specs=[flat_spec, flat_spec],
            out_specs=pair_spec,
            name="by_head",
        )(first, second)

    def exchange(x):
        return lax.all_to_all(x, spread, split_axis=0, concat_axis=0, tiled=True)

    def pair(own, sent):
        if n_t == 1:
            return own, jnp.zeros_like(sent)
        if n_t == 2:
            return own, lax.ppermute(sent, "t", [(0, 1), (1, 0)])
        return jnp.zeros_like(own), lax.psum(sent, "t")

    kv = exchange(by_head(key_tokens, values))
    by_column = learn_rates.T.reshape(n_s, n_head, rows)
    rates = []
    for j in range(n_s):
        piece = by_column[lax.rem(lax.axis_index("s") + j, n_s)]
        if j:
            piece = lax.ppermute(piece, "s", [(i, (i + j) % n_s) for i in range(n_s)])
        rates.append(piece)
    rate = pl.pallas_call(
        pack_rates_kernel,
        out_shape=jax.ShapeDtypeStruct((n_s * n_head, rows), F32),
        name="rate_pack",
    )(*rates)
    qo = exchange(by_head(queries, out_grad))

    per = blocks_per_step(pieces, rows, 1024)
    grid = (pieces // per,)
    two_spec = pl.BlockSpec((per, 2, rows, dim), lambda i, s: (i, 0, 0, 0))
    one_spec = pl.BlockSpec((per, rows, dim), lambda i, s: (i, 0, 0))
    rate_spec = pl.BlockSpec((n_s * n_head, rows), lambda i, s: (0, 0))
    w_spec = pl.BlockSpec((1, dim, dim), lambda i, s: (s[0], 0, 0))
    sum_spec = pl.BlockSpec((3, dim, dim), lambda i, s: (0, 0, 0))
    sum_shapes = [
        jax.ShapeDtypeStruct((3, dim, dim), F32),
        jax.ShapeDtypeStruct((3, dim, dim), BF16),
    ]
    params = pltpu.CompilerParams(
        dimension_semantics=("arbitrary",), vmem_limit_bytes=56 * 1024 * 1024
    )

    part, sent = pl.pallas_call(
        functools.partial(key_kernel, n_s),
        out_shape=sum_shapes,
        grid_spec=pltpu.PrefetchScalarGridSpec(
            num_scalar_prefetch=1,
            grid=grid,
            in_specs=[two_spec, rate_spec, w_spec, w_spec, w_spec],
            out_specs=[sum_spec, sum_spec],
        ),
        compiler_params=params,
        name="key_forward",
    )(place, kv, rate, w_gate, w_up, w_down)
    own, other = pair(part, sent)
    grad_q, part, sent = pl.pallas_call(
        functools.partial(query_kernel, scale),
        out_shape=[jax.ShapeDtypeStruct((pieces, rows, dim), BF16)] + sum_shapes,
        grid_spec=pltpu.PrefetchScalarGridSpec(
            num_scalar_prefetch=1,
            grid=grid,
            in_specs=[two_spec, w_spec, w_spec, w_spec, sum_spec, sum_spec],
            out_specs=[one_spec, sum_spec, sum_spec],
            scratch_shapes=[pltpu.VMEM((3, dim, dim), BF16)],
        ),
        compiler_params=params,
        name="query_side",
    )(place, qo, w_gate, w_up, w_down, own, other)
    own, other = pair(part, sent)
    grad_q = exchange(grad_q)
    grad_kv = pl.pallas_call(
        functools.partial(back_kernel, scale, n_s),
        out_shape=jax.ShapeDtypeStruct((pieces, 2, rows, dim), BF16),
        grid_spec=pltpu.PrefetchScalarGridSpec(
            num_scalar_prefetch=1,
            grid=grid,
            in_specs=[two_spec, rate_spec, w_spec, w_spec, w_spec, sum_spec, sum_spec],
            out_specs=two_spec,
            scratch_shapes=[pltpu.VMEM((3, dim, dim), BF16)],
        ),
        compiler_params=params,
        name="key_back",
    )(place, kv, rate, w_gate, w_up, w_down, own, other)
    grad_kv = exchange(grad_kv)
    grad_q = pl.pallas_call(
        home_one_kernel,
        out_shape=jax.ShapeDtypeStruct((rows, model), BF16),
        grid=copy_grid,
        in_specs=[pl.BlockSpec((heads, block, dim), lambda i: (0, i, 0))],
        out_specs=flat_spec,
        name="home_q",
    )(grad_q)
    grad_k, grad_v = pl.pallas_call(
        home_two_kernel,
        out_shape=[jax.ShapeDtypeStruct((rows, model), BF16)] * 2,
        grid=copy_grid,
        in_specs=[pair_spec],
        out_specs=[flat_spec, flat_spec],
        name="home_kv",
    )(grad_kv)
    return grad_q, grad_k, grad_v


def solution(mesh):
    n_tok, n_head = mesh.shape["tok"], mesh.shape["head"]

    def run(queries, key_tokens, values, out_grad, learn_rates, w_gate, w_up, w_down):
        n_s = w_gate.shape[0] // n_head
        n_t = n_tok // n_s
        split = Mesh(mesh.devices.reshape(n_t, n_s, n_head), ("t", "s", "head"))
        tokens = P(("t", "s", "head"), None)
        weights = P("head", None, None)
        return jax.shard_map(
            functools.partial(body, n_t, n_s, n_head),
            mesh=split,
            in_specs=(tokens,) * 4 + (P(("t", "s"), "head"),) + (weights,) * 3,
            out_specs=(tokens,) * 3,
            check_vma=False,
        )(queries, key_tokens, values, out_grad, learn_rates, w_gate, w_up, w_down)

    return run
```

```python
import functools
import math

import jax
import jax.numpy as jnp
from jax import lax
from jax.experimental import pallas as pl
from jax.experimental.pallas import tpu as pltpu
from jax.sharding import Mesh, PartitionSpec as P


F32 = jnp.float32
BF16 = jnp.bfloat16
HEADS_HELD = 2


def mm(a, b):
    return lax.dot_general(a, b, (((1,), (0,)), ((), ())), preferred_element_type=F32)


def mm_nt(a, b):
    return lax.dot_general(a, b, (((1,), (1,)), ((), ())), preferred_element_type=F32)


def mm_tn(a, b):
    return lax.dot_general(a, b, (((0,), (0,)), ((), ())), preferred_element_type=F32)


def sigmoid(x):
    return jax.nn.sigmoid(x)


def stack_kernel(at_ref, gate_ref, up_ref, down_ref, out_ref):
    dim = gate_ref.shape[-1]
    out_ref[0, :dim] = gate_ref[0]
    out_ref[0, dim : 2 * dim] = up_ref[0]
    out_ref[0, 2 * dim :] = down_ref[0]


def by_head_kernel(n_group, at_ref, *refs):
    for j in range(n_group):
        out_ref = refs[2 * n_group + j]
        out_ref[0] = refs[2 * j][...]
        out_ref[1] = refs[2 * j + 1][...]


def home_kernel(n_group, n_out, at_ref, *refs):
    outs = refs[-n_out:]
    dim = refs[0].shape[-1]
    for a in range(HEADS_HELD):
        for j in range(n_group):
            piece = refs[a * n_group + j]
            head = HEADS_HELD * jnp.bitwise_xor(at_ref[0], j) + a
            columns = pl.ds(pl.multiple_of(head * dim, dim), dim)
            if n_out == 1:
                outs[0][:, columns] = piece[...]
            else:
                for i, out in enumerate(outs):
                    out[:, columns] = piece[i]


def tall_rates(at_ref, rate_refs, n_group, dim):
    n_s = len(rate_refs)
    head = at_ref[0] // n_s
    columns = []
    for j in range(n_group):
        ref = rate_refs[j % n_s]
        row = ref[0, pl.ds(jnp.bitwise_xor(head, j // n_s), 1), :]
        columns.append(jnp.broadcast_to(row, (128, row.shape[1])).T)
    tall = jnp.concatenate(columns, axis=0)
    return jnp.concatenate([tall] * (dim // 128), axis=1)


def stacked(refs, which):
    return jnp.concatenate([ref[which] for ref in refs], axis=0)


def hand_out(at_ref, acc, own_ref, sent_refs):
    rows = own_ref.shape[0]
    n_chunk = len(sent_refs) + 1
    for j, ref in enumerate((own_ref,) + tuple(sent_refs)):
        start = jnp.bitwise_xor(at_ref[1], j) * rows if n_chunk > 1 else 0
        chunk = acc[pl.ds(pl.multiple_of(start, 16), rows), :]
        ref[...] = chunk.astype(ref.dtype)


def take_in(at_ref, chunk_refs, whole):
    rows = chunk_refs[0].shape[0]
    for j, ref in enumerate(chunk_refs):
        start = jnp.bitwise_xor(at_ref[1], j) * rows if len(chunk_refs) > 1 else 0
        whole[pl.ds(pl.multiple_of(start, 16), rows), :] = ref[...]


def key_kernel(n_group, n_s, n_chunk, at_ref, *refs):
    pieces, refs = refs[:n_group], refs[n_group:]
    rate_refs, refs = refs[:n_s], refs[n_s:]
    w_ref, refs = refs[0], refs[1:]
    own_ref, sent_refs, acc = refs[-n_chunk - 1], refs[-n_chunk:-1], refs[-1]
    step = pl.program_id(0)
    dim = pieces[0].shape[-1]

    @pl.when(step == 0)
    def _():
        acc[...] = jnp.zeros_like(acc)

    k = stacked(pieces, 0)
    rate = tall_rates(at_ref, rate_refs, n_group, dim)
    scaled = (rate * stacked(pieces, 1).astype(F32)).astype(BF16)
    gate = mm(k, w_ref[0, :dim])
    up = mm(k, w_ref[0, dim : 2 * dim])
    dhid = mm_nt(scaled, w_ref[0, 2 * dim :])
    sig = sigmoid(gate)
    act = gate * sig
    hidden = (act * up).astype(BF16)
    dgate = (dhid * up * (sig * (1.0 + gate * (1.0 - sig)))).astype(BF16)
    dup = (dhid * act).astype(BF16)
    acc[:dim] += mm_tn(k, dgate)
    acc[dim : 2 * dim] += mm_tn(k, dup)
    acc[2 * dim :] += mm_tn(hidden, scaled)

    @pl.when(step == pl.num_programs(0) - 1)
    def _():
        hand_out(at_ref, acc, own_ref, sent_refs)


def fresh_kernel(scale, n_chunk, at_ref, own_ref, *refs):
    total = own_ref[...]
    for ref in refs[: n_chunk - 1]:
        total = total + ref[...].astype(F32)
    w_ref, out_ref = refs[n_chunk - 1], refs[-1]
    out_ref[...] = (w_ref[0].astype(F32) + scale * total).astype(BF16)


def adjoint_kernel(scale, n_chunk, at_ref, own_ref, *refs):
    total = own_ref[...]
    for ref in refs[: n_chunk - 1]:
        total = total + ref[...].astype(F32)
    refs[-1][...] = (scale * total).astype(BF16)


def query_kernel(n_group, n_chunk, at_ref, *refs):
    pieces, refs = refs[:n_group], refs[n_group:]
    chunk_refs = refs[:n_chunk]
    acc, fresh = refs[-2:]
    refs = refs[:-2]
    own_ref, sent_refs = refs[-n_chunk], refs[len(refs) - n_chunk + 1 :]
    grads = refs[-n_chunk - n_group : -n_chunk]
    step = pl.program_id(0)
    dim = pieces[0].shape[-1]

    @pl.when(step == 0)
    def _():
        acc[...] = jnp.zeros_like(acc)
        take_in(at_ref, chunk_refs, fresh)

    q = stacked(pieces, 0)
    o = stacked(pieces, 1)
    w_gate, w_up, w_down = fresh[:dim], fresh[dim : 2 * dim], fresh[2 * dim :]
    gate = mm(q, w_gate)
    up = mm(q, w_up)
    dhid = mm_nt(o, w_down)
    sig = sigmoid(gate)
    act = gate * sig
    hidden = (act * up).astype(BF16)
    dgate = (dhid * up * (sig * (1.0 + gate * (1.0 - sig)))).astype(BF16)
    dup = (dhid * act).astype(BF16)
    grad = (mm_nt(dgate, w_gate) + mm_nt(dup, w_up)).astype(BF16)
    rows = grads[0].shape[0]
    for j, ref in enumerate(grads):
        ref[...] = grad[j * rows : (j + 1) * rows]
    acc[:dim] += mm_tn(q, dgate)
    acc[dim : 2 * dim] += mm_tn(q, dup)
    acc[2 * dim :] += mm_tn(hidden, o)

    @pl.when(step == pl.num_programs(0) - 1)
    def _():
        hand_out(at_ref, acc, own_ref, sent_refs)


def back_kernel(n_group, n_s, n_chunk, at_ref, *refs):
    pieces, refs = refs[:n_group], refs[n_group:]
    rate_refs, refs = refs[:n_s], refs[n_s:]
    w_ref, chunk_refs, adj = refs[0], refs[1 : n_chunk + 1], refs[-1]
    outs = refs[-n_group - 1 : -1]
    dim = pieces[0].shape[-1]

    @pl.when(pl.program_id(0) == 0)
    def _():
        take_in(at_ref, chunk_refs, adj)

    k = stacked(pieces, 0)
    rate = tall_rates(at_ref, rate_refs, n_group, dim)
    scaled = (rate * stacked(pieces, 1).astype(F32)).astype(BF16)
    w_gate, w_up, w_down = w_ref[0, :dim], w_ref[0, dim : 2 * dim], w_ref[0, 2 * dim :]
    adj_gate, adj_up, adj_down = adj[:dim], adj[dim : 2 * dim], adj[2 * dim :]
    gate = mm(k, w_gate)
    up = mm(k, w_up)
    dhid = mm_nt(scaled, w_down)
    sig = sigmoid(gate)
    act = gate * sig
    rest = 1.0 - sig
    slope = sig * (1.0 + gate * rest)
    curve = sig * rest * (2.0 + gate * (1.0 - 2.0 * sig))
    hidden = (act * up).astype(BF16)
    dgate = (dhid * up * slope).astype(BF16)
    dup = (dhid * act).astype(BF16)
    back_dgate = mm(k, adj_gate)
    back_dup = mm(k, adj_up)
    back_hidden = mm_nt(scaled, adj_down)
    back_scaled = mm(hidden, adj_down)
    back_dhid = (back_dgate * up * slope + back_dup * act).astype(BF16)
    back_gate = (
        back_dgate * dhid * up * curve + (back_dup * dhid + back_hidden * up) * slope
    ).astype(BF16)
    back_upper = (back_dgate * dhid * slope + back_hidden * act).astype(BF16)
    grad_k = mm_nt(dgate, adj_gate) + mm_nt(dup, adj_up)
    grad_k = (grad_k + mm_nt(back_gate, w_gate) + mm_nt(back_upper, w_up)).astype(BF16)
    grad_v = (rate * (back_scaled + mm(back_dhid, w_down))).astype(BF16)
    rows = outs[0].shape[1]
    for j, ref in enumerate(outs):
        ref[0] = grad_k[j * rows : (j + 1) * rows]
        ref[1] = grad_v[j * rows : (j + 1) * rows]


def body(n_t, n_s, n_head, queries, key_tokens, values, out_grad, learn_rates, w_gate, w_up, w_down):
    rows, model = queries.shape
    n_group = n_head * n_s
    dim = model // (n_group * HEADS_HELD)
    held = range(HEADS_HELD)
    n_chunk = n_t if n_t in (2, 4) else 1
    part = 3 * dim // n_chunk
    tile = min(rows, 128)
    grid = (rows // tile,)
    scale = 1.0 / math.sqrt(dim * rows * n_group * n_t)
    place = lax.axis_index("head") * n_s + lax.axis_index("s")
    at = jnp.stack([place, lax.axis_index("t")]).astype(jnp.int32)

    def partners(j):
        pairs = []
        for g in range(n_group):
            ends = [(x % n_s) * n_head + x // n_s for x in (g, g ^ j)]
            pairs.append(tuple(ends))
        return pairs

    params = pltpu.CompilerParams(
        dimension_semantics=("arbitrary",), vmem_limit_bytes=56 * 1024 * 1024
    )
    free = pl.BlockSpec(memory_space=pl.ANY)

    def call(kernel, grid, in_specs, out_specs, out_shape, scratch, *args, after=()):
        n_in = len(args)
        if after:
            inner = kernel

            def kernel(*refs):
                inner(*refs[: n_in + 1], *refs[n_in + 1 + len(after) :])

        return pl.pallas_call(
            kernel,
            out_shape=out_shape,
            grid_spec=pltpu.PrefetchScalarGridSpec(
                num_scalar_prefetch=1,
                grid=grid,
                in_specs=list(in_specs) + [free] * len(after),
                out_specs=out_specs,
                scratch_shapes=scratch,
            ),
            compiler_params=params,
        )(at, *args, *after)

    def by_head(first, second, a, after=()):
        specs = []
        for j in range(n_group):
            spec = pl.BlockSpec(
                (tile, dim), lambda i, p, j=j: (i, HEADS_HELD * jnp.bitwise_xor(p[0], j) + a)
            )
            specs += [spec, spec]
        return call(
            functools.partial(by_head_kernel, n_group),
            grid,
            specs,
            [pl.BlockSpec((2, tile, dim), lambda i, p: (0, i, 0))] * n_group,
            [jax.ShapeDtypeStruct((2, rows, dim), BF16)] * n_group,
            [],
            *([first, second] * n_group),
            after=after,
        )

    def swap(pieces):
        return [pieces[0]] + [
            lax.ppermute(pieces[j], ("s", "head"), partners(j))
            for j in range(1, n_group)
        ]

    def scatter(own, sent):
        if n_chunk == 1:
            return [lax.psum(own, "t") if n_t > 1 else own]
        return [own] + [
            lax.ppermute(sent[j - 1], "t", [(i, i ^ j) for i in range(n_t)])
            for j in range(1, n_chunk)
        ]

    def gather(chunk):
        return [chunk] + [
            lax.ppermute(chunk, "t", [(i, i ^ j) for i in range(n_t)])
            for j in range(1, n_chunk)
        ]

    piece_specs = [pl.BlockSpec((2, tile, dim), lambda i, p: (0, i, 0))] * n_group
    chunk_spec = pl.BlockSpec((part, dim), lambda i, p: (0, 0))
    chunk_shapes = [jax.ShapeDtypeStruct((part, dim), F32)]
    chunk_shapes += [jax.ShapeDtypeStruct((part, dim), BF16)] * (n_chunk - 1)
    whole = (3 * dim, dim)

    def rate_specs(a):
        return [pl.BlockSpec((1, n_head, tile), lambda i, p: (a, 0, i))] * n_s

    def w_spec(a):
        return pl.BlockSpec((1,) + whole, lambda i, p: (a, 0, 0))

    kv, qo = [None] * HEADS_HELD, [None] * HEADS_HELD
    last = ()
    for a in held:
        pieces = by_head(key_tokens, values, a, after=last)
        kv[a] = swap(pieces)
        last = (pieces[0],)
    by_column = learn_rates.T.reshape(n_s, HEADS_HELD, n_head, rows)
    rates = []
    for j in range(n_s):
        piece = by_column[jnp.bitwise_xor(lax.axis_index("s"), j)]
        if j:
            piece = lax.ppermute(piece, "s", [(i, i ^ j) for i in range(n_s)])
        rates.append(piece)
    for a in held:
        pieces = by_head(queries, out_grad, a, after=last)
        qo[a] = swap(pieces)
        last = (pieces[0],)

    first_spec = pl.BlockSpec(
        (1, dim, dim), lambda i, p: (HEADS_HELD * lax.rem(p[0], n_s) + i, 0, 0)
    )
    w = call(
        stack_kernel,
        (HEADS_HELD,),
        [first_spec] * 3,
        pl.BlockSpec((1,) + whole, lambda i, p: (i, 0, 0)),
        jax.ShapeDtypeStruct((HEADS_HELD,) + whole, BF16),
        [],
        w_gate,
        w_up,
        w_down,
        after=last,
    )

    def key_forward(a, after=()):
        own, *sent = call(
            functools.partial(key_kernel, n_group, n_s, n_chunk),
            grid,
            piece_specs + rate_specs(a) + [w_spec(a)],
            [chunk_spec] * n_chunk,
            chunk_shapes,
            [pltpu.VMEM(whole, F32)],
            *kv[a],
            *rates,
            w,
            after=after,
        )
        return own, scatter(own, sent)

    def make_fresh(a, chunks, after=()):
        out = call(
            functools.partial(fresh_kernel, scale, n_chunk),
            (1,),
            [chunk_spec] * n_chunk
            + [pl.BlockSpec((1, part, dim), lambda i, p: (a, p[1] if n_chunk > 1 else 0, 0))],
            chunk_spec,
            jax.ShapeDtypeStruct((part, dim), BF16),
            [],
            *chunks,
            w,
            after=after,
        )
        return out, gather(out)

    def query_side(a, fresh, after=()):
        outs = call(
            functools.partial(query_kernel, n_group, n_chunk),
            grid,
            piece_specs + [chunk_spec] * n_chunk,
            [pl.BlockSpec((tile, dim), lambda i, p: (i, 0))] * n_group + [chunk_spec] * n_chunk,
            [jax.ShapeDtypeStruct((rows, dim), BF16)] * n_group + chunk_shapes,
            [pltpu.VMEM(whole, F32), pltpu.VMEM(whole, BF16)],
            *qo[a],
            *fresh,
            after=after,
        )
        grads, own, sent = outs[:n_group], outs[n_group], outs[n_group + 1 :]
        chunks = scatter(own, sent)
        return own, chunks, swap(grads)

    def make_adjoint(chunks, after=()):
        out = call(
            functools.partial(adjoint_kernel, scale, n_chunk),
            (1,),
            [chunk_spec] * n_chunk,
            chunk_spec,
            jax.ShapeDtypeStruct((part, dim), BF16),
            [],
            *chunks,
            after=after,
        )
        return out, gather(out)

    def key_back(a, adjoint, after=()):
        outs = call(
            functools.partial(back_kernel, n_group, n_s, n_chunk),
            grid,
            piece_specs + rate_specs(a) + [w_spec(a)] + [chunk_spec] * n_chunk,
            piece_specs,
            [jax.ShapeDtypeStruct((2, rows, dim), BF16)] * n_group,
            [pltpu.VMEM(whole, BF16)],
            *kv[a],
            *rates,
            w,
            *adjoint,
            after=after,
        )
        return outs[0], swap(outs)

    mark, chunks_a = key_forward(0)
    mark, chunks_b = key_forward(1, (mark,))
    mark, fresh_a = make_fresh(0, chunks_a, (mark,))
    mark, fresh_b = make_fresh(1, chunks_b, (mark,))
    mark, sums_a, gq_a = query_side(0, fresh_a, (mark,))
    mark, adjoint_a = make_adjoint(sums_a, (mark,))
    mark, sums_b, gq_b = query_side(1, fresh_b, (mark,))
    mark, gkv_a = key_back(0, adjoint_a, (mark,))
    mark, adjoint_b = make_adjoint(sums_b, (mark,))
    mark, gkv_b = key_back(1, adjoint_b, (mark,))
    flat_spec = pl.BlockSpec((tile, model), lambda i, p: (i, 0))
    flat_shape = jax.ShapeDtypeStruct((rows, model), BF16)
    grad_q = call(
        functools.partial(home_kernel, n_group, 1),
        grid,
        [pl.BlockSpec((tile, dim), lambda i, p: (i, 0))] * (2 * n_group),
        [flat_spec],
        [flat_shape],
        [],
        *gq_a,
        *gq_b,
        after=(mark,),
    )[0]
    grad_k, grad_v = call(
        functools.partial(home_kernel, n_group, 2),
        grid,
        piece_specs * 2,
        [flat_spec] * 2,
        [flat_shape] * 2,
        [],
        *gkv_a,
        *gkv_b,
    )
    return grad_q, grad_k, grad_v


def solution(mesh):
    n_tok, n_head = mesh.shape["tok"], mesh.shape["head"]

    def run(queries, key_tokens, values, out_grad, learn_rates, w_gate, w_up, w_down):
        n_s = w_gate.shape[0] // (n_head * HEADS_HELD)
        n_t = n_tok // n_s
        split = Mesh(mesh.devices.reshape(n_t, n_s, n_head), ("t", "s", "head"))
        tokens = P(("t", "s", "head"), None)
        weights = P("head", None, None)
        return jax.shard_map(
            functools.partial(body, n_t, n_s, n_head),
            mesh=split,
            in_specs=(tokens,) * 4 + (P(("t", "s"), "head"),) + (weights,) * 3,
            out_specs=(tokens,) * 3,
            check_vma=False,
        )(queries, key_tokens, values, out_grad, learn_rates, w_gate, w_up, w_down)


    return run
```

```python
import functools
import math

import jax
import jax.numpy as jnp
from jax import lax
from jax.experimental import pallas as pl
from jax.experimental.pallas import tpu as pltpu
from jax.sharding import Mesh, PartitionSpec as P


F32 = jnp.float32
BF16 = jnp.bfloat16
HEADS_HELD = 2


def mm(a, b):
    return lax.dot_general(a, b, (((1,), (0,)), ((), ())), preferred_element_type=F32)


def mm_nt(a, b):
    return lax.dot_general(a, b, (((1,), (1,)), ((), ())), preferred_element_type=F32)


def mm_tn(a, b):
    return lax.dot_general(a, b, (((0,), (0,)), ((), ())), preferred_element_type=F32)


def sigmoid(x):
    return jax.nn.sigmoid(x)


def by_head_kernel(n_group, at_ref, first_ref, second_ref, *outs):
    dim = outs[0].shape[-1]
    for a in range(HEADS_HELD):
        for j in range(n_group):
            head = HEADS_HELD * jnp.bitwise_xor(at_ref[0], j) + a
            columns = pl.ds(pl.multiple_of(head * dim, dim), dim)
            outs[a * n_group + j][0] = first_ref[:, columns]
            outs[a * n_group + j][1] = second_ref[:, columns]


def home_kernel(n_group, n_out, at_ref, *refs):
    outs = refs[-n_out:]
    dim = refs[0].shape[-1]
    for a in range(HEADS_HELD):
        for j in range(n_group):
            piece = refs[a * n_group + j]
            head = HEADS_HELD * jnp.bitwise_xor(at_ref[0], j) + a
            columns = pl.ds(pl.multiple_of(head * dim, dim), dim)
            if n_out == 1:
                outs[0][:, columns] = piece[...]
            else:
                for i, out in enumerate(outs):
                    out[:, columns] = piece[i]


def tall_rates(at_ref, rate_refs, n_group, dim):
    n_s = len(rate_refs)
    head = at_ref[0] // n_s
    columns = []
    for j in range(n_group):
        ref = rate_refs[j % n_s]
        row = ref[0, pl.ds(jnp.bitwise_xor(head, j // n_s), 1), :]
        columns.append(jnp.broadcast_to(row, (128, row.shape[1])).T)
    tall = jnp.concatenate(columns, axis=0)
    return jnp.concatenate([tall] * (dim // 128), axis=1)


def stacked(refs, which):
    return jnp.concatenate([ref[which] for ref in refs], axis=0)


def total_of(own_ref, other_refs):
    total = own_ref[...]
    for ref in other_refs:
        total = total + ref[...].astype(F32)
    return total


def key_kernel(n_group, n_s, at_ref, *refs):
    pieces, refs = refs[:n_group], refs[n_group:]
    rate_refs, refs = refs[:n_s], refs[n_s:]
    wg_ref, wu_ref, wd_ref, acc, sent_ref = refs
    step = pl.program_id(0)
    dim = pieces[0].shape[-1]

    @pl.when(step == 0)
    def _():
        acc[...] = jnp.zeros_like(acc)

    k = stacked(pieces, 0)
    rate = tall_rates(at_ref, rate_refs, n_group, dim)
    scaled = (rate * stacked(pieces, 1).astype(F32)).astype(BF16)
    gate = mm(k, wg_ref[0])
    up = mm(k, wu_ref[0])
    dhid = mm_nt(scaled, wd_ref[0])
    sig = sigmoid(gate)
    act = gate * sig
    hidden = (act * up).astype(BF16)
    dgate = (dhid * up * (sig * (1.0 + gate * (1.0 - sig)))).astype(BF16)
    dup = (dhid * act).astype(BF16)
    acc[:dim] += mm_tn(k, dgate)
    acc[dim : 2 * dim] += mm_tn(k, dup)
    acc[2 * dim :] += mm_tn(hidden, scaled)

    @pl.when(step == pl.num_programs(0) - 1)
    def _():
        sent_ref[...] = acc[...].astype(BF16)


def query_kernel(scale, n_group, n_other, at_ref, *refs):
    pieces, refs = refs[:n_group], refs[n_group:]
    w_refs, own_ref, other_refs = refs[:3], refs[3], refs[4 : 4 + n_other]
    refs = refs[4 + n_other :]
    grads, acc, sent_ref, fresh = refs[:n_group], refs[-3], refs[-2], refs[-1]
    step = pl.program_id(0)
    dim = pieces[0].shape[-1]

    @pl.when(step == 0)
    def _():
        acc[...] = jnp.zeros_like(acc)
        total = total_of(own_ref, other_refs)
        for i, ref in enumerate(w_refs):
            rows = slice(i * dim, (i + 1) * dim)
            fresh[rows] = (ref[0].astype(F32) + scale * total[rows]).astype(BF16)

    q = stacked(pieces, 0)
    o = stacked(pieces, 1)
    w_gate, w_up, w_down = fresh[:dim], fresh[dim : 2 * dim], fresh[2 * dim :]
    gate = mm(q, w_gate)
    up = mm(q, w_up)
    dhid = mm_nt(o, w_down)
    sig = sigmoid(gate)
    act = gate * sig
    hidden = (act * up).astype(BF16)
    dgate = (dhid * up * (sig * (1.0 + gate * (1.0 - sig)))).astype(BF16)
    dup = (dhid * act).astype(BF16)
    grad = (mm_nt(dgate, w_gate) + mm_nt(dup, w_up)).astype(BF16)
    rows = grads[0].shape[0]
    for j, ref in enumerate(grads):
        ref[...] = grad[j * rows : (j + 1) * rows]
    acc[:dim] += mm_tn(q, dgate)
    acc[dim : 2 * dim] += mm_tn(q, dup)
    acc[2 * dim :] += mm_tn(hidden, o)

    @pl.when(step == pl.num_programs(0) - 1)
    def _():
        sent_ref[...] = acc[...].astype(BF16)


def back_kernel(scale, n_group, n_s, n_other, at_ref, *refs):
    pieces, refs = refs[:n_group], refs[n_group:]
    rate_refs, refs = refs[:n_s], refs[n_s:]
    w_gate, w_up, w_down = (ref[0] for ref in refs[:3])
    own_ref, other_refs = refs[3], refs[4 : 4 + n_other]
    outs, adj = refs[4 + n_other : -1], refs[-1]
    dim = pieces[0].shape[-1]

    @pl.when(pl.program_id(0) == 0)
    def _():
        adj[...] = (scale * total_of(own_ref, other_refs)).astype(BF16)

    k = stacked(pieces, 0)
    rate = tall_rates(at_ref, rate_refs, n_group, dim)
    scaled = (rate * stacked(pieces, 1).astype(F32)).astype(BF16)
    adj_gate, adj_up, adj_down = adj[:dim], adj[dim : 2 * dim], adj[2 * dim :]
    gate = mm(k, w_gate)
    up = mm(k, w_up)
    dhid = mm_nt(scaled, w_down)
    sig = sigmoid(gate)
    act = gate * sig
    rest = 1.0 - sig
    slope = sig * (1.0 + gate * rest)
    curve = sig * rest * (2.0 + gate * (1.0 - 2.0 * sig))
    hidden = (act * up).astype(BF16)
    dgate = (dhid * up * slope).astype(BF16)
    dup = (dhid * act).astype(BF16)
    back_dgate = mm(k, adj_gate)
    back_dup = mm(k, adj_up)
    back_hidden = mm_nt(scaled, adj_down)
    back_scaled = mm(hidden, adj_down)
    back_dhid = (back_dgate * up * slope + back_dup * act).astype(BF16)
    back_gate = (
        back_dgate * dhid * up * curve + (back_dup * dhid + back_hidden * up) * slope
    ).astype(BF16)
    back_upper = (back_dgate * dhid * slope + back_hidden * act).astype(BF16)
    grad_k = mm_nt(dgate, adj_gate) + mm_nt(dup, adj_up)
    grad_k = (grad_k + mm_nt(back_gate, w_gate) + mm_nt(back_upper, w_up)).astype(BF16)
    grad_v = (rate * (back_scaled + mm(back_dhid, w_down))).astype(BF16)
    rows = outs[0].shape[1]
    for j, ref in enumerate(outs):
        ref[0] = grad_k[j * rows : (j + 1) * rows]
        ref[1] = grad_v[j * rows : (j + 1) * rows]


def body(n_t, n_s, n_head, queries, key_tokens, values, out_grad, learn_rates, w_gate, w_up, w_down):
    rows, model = queries.shape
    n_group = n_head * n_s
    dim = model // (n_group * HEADS_HELD)
    held = range(HEADS_HELD)
    hops = [1 << i for i in range(n_t.bit_length() - 1)] if n_t & (n_t - 1) == 0 else None
    tile = min(rows, 128)
    grid = (rows // tile,)
    scale = 1.0 / math.sqrt(dim * rows * n_group * n_t)
    place = lax.axis_index("head") * n_s + lax.axis_index("s")
    at = jnp.stack([place, lax.axis_index("t")]).astype(jnp.int32)

    def partners(j):
        pairs = []
        for g in range(n_group):
            ends = [(x % n_s) * n_head + x // n_s for x in (g, g ^ j)]
            pairs.append(tuple(ends))
        return pairs

    params = pltpu.CompilerParams(
        dimension_semantics=("arbitrary",), vmem_limit_bytes=56 * 1024 * 1024
    )
    free = pl.BlockSpec(memory_space=pl.ANY)

    def call(kernel, grid, in_specs, out_specs, out_shape, scratch, *args, after=()):
        n_in = len(args)
        if after:
            inner = kernel

            def kernel(*refs):
                inner(*refs[: n_in + 1], *refs[n_in + 1 + len(after) :])

        return pl.pallas_call(
            kernel,
            out_shape=out_shape,
            grid_spec=pltpu.PrefetchScalarGridSpec(
                num_scalar_prefetch=1,
                grid=grid,
                in_specs=list(in_specs) + [free] * len(after),
                out_specs=out_specs,
                scratch_shapes=scratch,
            ),
            compiler_params=params,
        )(at, *args, *after)

    flat_spec = pl.BlockSpec((tile, model), lambda i, p: (i, 0))
    flat_shape = jax.ShapeDtypeStruct((rows, model), BF16)
    piece_specs = [pl.BlockSpec((2, tile, dim), lambda i, p: (0, i, 0))] * n_group

    def by_head(first, second):
        outs = call(
            functools.partial(by_head_kernel, n_group),
            grid,
            [flat_spec, flat_spec],
            piece_specs * HEADS_HELD,
            [jax.ShapeDtypeStruct((2, rows, dim), BF16)] * (n_group * HEADS_HELD),
            [],
            first,
            second,
        )
        return [outs[a * n_group : (a + 1) * n_group] for a in held]

    def swap(pieces):
        return [pieces[0]] + [
            lax.ppermute(pieces[j], ("s", "head"), partners(j))
            for j in range(1, n_group)
        ]

    def reduce(own, sent):
        if hops is None:
            return own, [lax.psum(sent, "t")]
        others = []
        for i, hop in enumerate(hops):
            if i:
                own = own + others.pop().astype(F32)
                sent = own.astype(BF16)
            others.append(lax.ppermute(sent, "t", [(j, j ^ hop) for j in range(n_t)]))
        return own, others

    sum_spec = pl.BlockSpec((3 * dim, dim), lambda i, p: (0, 0))
    sum_specs = [sum_spec, sum_spec]
    sum_shapes = [
        jax.ShapeDtypeStruct((3 * dim, dim), F32),
        jax.ShapeDtypeStruct((3 * dim, dim), BF16),
    ]

    def rate_specs(a):
        return [pl.BlockSpec((1, n_head, tile), lambda i, p: (a, 0, i))] * n_s

    def w_specs(a):
        spec = pl.BlockSpec(
            (1, dim, dim), lambda i, p: (HEADS_HELD * lax.rem(p[0], n_s) + a, 0, 0)
        )
        return [spec] * 3

    weights = (w_gate, w_up, w_down)
    kv = by_head(key_tokens, values)
    kv = [swap(kv[a]) for a in held]
    by_column = learn_rates.T.reshape(n_s, HEADS_HELD, n_head, rows)
    rates = []
    for j in range(n_s):
        piece = by_column[jnp.bitwise_xor(lax.axis_index("s"), j)]
        if j:
            piece = lax.ppermute(piece, "s", [(i, i ^ j) for i in range(n_s)])
        rates.append(piece)
    qo = by_head(queries, out_grad)
    qo = [swap(qo[a]) for a in held]

    def key_forward(a, after=()):
        own, sent = call(
            functools.partial(key_kernel, n_group, n_s),
            grid,
            piece_specs + rate_specs(a) + w_specs(a),
            sum_specs,
            sum_shapes,
            [],
            *kv[a],
            *rates,
            *weights,
            after=after,
        )
        return own, reduce(own, sent)

    def query_side(a, own, others, after=()):
        outs = call(
            functools.partial(query_kernel, scale, n_group, len(others)),
            grid,
            piece_specs + w_specs(a) + [sum_spec] * (1 + len(others)),
            [pl.BlockSpec((tile, dim), lambda i, p: (i, 0))] * n_group + sum_specs,
            [jax.ShapeDtypeStruct((rows, dim), BF16)] * n_group + sum_shapes,
            [pltpu.VMEM((3 * dim, dim), BF16)],
            *qo[a],
            *weights,
            own,
            *others,
            after=after,
        )
        grads, own, sent = outs[:n_group], outs[n_group], outs[n_group + 1]
        return own, reduce(own, sent), swap(grads)

    def key_back(a, own, others, after=()):
        outs = call(
            functools.partial(back_kernel, scale, n_group, n_s, len(others)),
            grid,
            piece_specs + rate_specs(a) + w_specs(a) + [sum_spec] * (1 + len(others)),
            piece_specs,
            [jax.ShapeDtypeStruct((2, rows, dim), BF16)] * n_group,
            [pltpu.VMEM((3 * dim, dim), BF16)],
            *kv[a],
            *rates,
            *weights,
            own,
            *others,
            after=after,
        )
        return outs[0], swap(outs)

    delta, sums, gq, gkv = ([None] * HEADS_HELD for _ in range(4))
    mark = ()
    for a in held:
        mark, delta[a] = key_forward(a, mark)
        mark = (mark,)
    for a in held:
        mark, sums[a], gq[a] = query_side(a, *delta[a], mark)
        mark = (mark,)
    for a in held:
        mark, gkv[a] = key_back(a, *sums[a], mark)
        mark = (mark,)
    grad_q = call(
        functools.partial(home_kernel, n_group, 1),
        grid,
        [pl.BlockSpec((tile, dim), lambda i, p: (i, 0))] * (HEADS_HELD * n_group),
        [flat_spec],
        [flat_shape],
        [],
        *gq[0],
        *gq[1],
        after=mark,
    )[0]
    grad_k, grad_v = call(
        functools.partial(home_kernel, n_group, 2),
        grid,
        piece_specs * HEADS_HELD,
        [flat_spec] * 2,
        [flat_shape] * 2,
        [],
        *gkv[0],
        *gkv[1],
    )
    return grad_q, grad_k, grad_v


def solution(mesh):
    n_tok, n_head = mesh.shape["tok"], mesh.shape["head"]

    def run(queries, key_tokens, values, out_grad, learn_rates, w_gate, w_up, w_down):
        n_s = w_gate.shape[0] // (n_head * HEADS_HELD)
        n_t = n_tok // n_s
        split = Mesh(mesh.devices.reshape(n_t, n_s, n_head), ("t", "s", "head"))
        tokens = P(("t", "s", "head"), None)
        weights = P("head", None, None)
        return jax.shard_map(
            functools.partial(body, n_t, n_s, n_head),
            mesh=split,
            in_specs=(tokens,) * 4 + (P(("t", "s"), "head"),) + (weights,) * 3,
            out_specs=(tokens,) * 3,
            check_vma=False,
        )(queries, key_tokens, values, out_grad, learn_rates, w_gate, w_up, w_down)


    return run
```

```python
import functools
import math

import jax
import jax.numpy as jnp
from jax import lax
from jax.experimental import pallas as pl
from jax.experimental.pallas import tpu as pltpu
from jax.sharding import Mesh, PartitionSpec as P


F32 = jnp.float32
BF16 = jnp.bfloat16
HEADS_HELD = 2


def mm(a, b):
    return lax.dot_general(a, b, (((1,), (0,)), ((), ())), preferred_element_type=F32)


def mm_nt(a, b):
    return lax.dot_general(a, b, (((1,), (1,)), ((), ())), preferred_element_type=F32)


def mm_tn(a, b):
    return lax.dot_general(a, b, (((0,), (0,)), ((), ())), preferred_element_type=F32)


def sigmoid(x):
    return jax.nn.sigmoid(x)


def by_head_kernel(n_group, at_ref, first_ref, second_ref, *outs):
    dim = outs[0].shape[-1]
    for a in range(HEADS_HELD):
        for j in range(n_group):
            head = HEADS_HELD * jnp.bitwise_xor(at_ref[0], j) + a
            columns = pl.ds(pl.multiple_of(head * dim, dim), dim)
            outs[a * n_group + j][0] = first_ref[:, columns]
            outs[a * n_group + j][1] = second_ref[:, columns]


def home_kernel(n_group, n_out, at_ref, *refs):
    outs = refs[-n_out:]
    dim = refs[0].shape[-1]
    for a in range(HEADS_HELD):
        for j in range(n_group):
            piece = refs[a * n_group + j]
            head = HEADS_HELD * jnp.bitwise_xor(at_ref[0], j) + a
            columns = pl.ds(pl.multiple_of(head * dim, dim), dim)
            if n_out == 1:
                outs[0][:, columns] = piece[...]
            else:
                for i, out in enumerate(outs):
                    out[:, columns] = piece[i]


def fill_rates(at_ref, rate_refs, tall):
    n_s = len(rate_refs)
    head = at_ref[0] // n_s
    for j in range(tall.shape[0]):
        ref = rate_refs[j % n_s]
        row = ref[0, pl.ds(jnp.bitwise_xor(head, j // n_s), 1), :]
        tall[j] = jnp.broadcast_to(row, (tall.shape[2], row.shape[1])).T


def tall_rates(tall, rows, dim):
    start = pl.multiple_of(pl.program_id(0) * rows, rows)
    column = jnp.concatenate([tall[j, pl.ds(start, rows)] for j in range(tall.shape[0])], axis=0)
    return jnp.concatenate([column] * (dim // tall.shape[2]), axis=1)


def stacked(refs, which):
    return jnp.concatenate([ref[which] for ref in refs], axis=0)


def total_of(own_ref, other_refs):
    total = own_ref[...]
    for ref in other_refs:
        total = total + ref[...].astype(F32)
    return total


def key_kernel(n_group, n_s, at_ref, *refs):
    pieces, refs = refs[:n_group], refs[n_group:]
    rate_refs, refs = refs[:n_s], refs[n_s:]
    wg_ref, wu_ref, wd_ref, acc, sent_ref, tall = refs
    step = pl.program_id(0)
    dim = pieces[0].shape[-1]

    @pl.when(step == 0)
    def _():
        acc[...] = jnp.zeros_like(acc)
        fill_rates(at_ref, rate_refs, tall)

    k = stacked(pieces, 0)
    rate = tall_rates(tall, pieces[0].shape[1], dim)
    scaled = (rate * stacked(pieces, 1).astype(F32)).astype(BF16)
    gate = mm(k, wg_ref[0])
    up = mm(k, wu_ref[0])
    dhid = mm_nt(scaled, wd_ref[0])
    sig = sigmoid(gate)
    act = gate * sig
    hidden = (act * up).astype(BF16)
    dgate = (dhid * up * (sig * (1.0 + gate * (1.0 - sig)))).astype(BF16)
    dup = (dhid * act).astype(BF16)
    acc[:dim] += mm_tn(k, dgate)
    acc[dim : 2 * dim] += mm_tn(k, dup)
    acc[2 * dim :] += mm_tn(hidden, scaled)

    @pl.when(step == pl.num_programs(0) - 1)
    def _():
        sent_ref[...] = acc[...].astype(BF16)


def query_kernel(scale, n_group, n_other, at_ref, *refs):
    pieces, refs = refs[:n_group], refs[n_group:]
    w_refs, own_ref, other_refs = refs[:3], refs[3], refs[4 : 4 + n_other]
    refs = refs[4 + n_other :]
    grads, acc, sent_ref, fresh = refs[:n_group], refs[-3], refs[-2], refs[-1]
    step = pl.program_id(0)
    dim = pieces[0].shape[-1]

    @pl.when(step == 0)
    def _():
        acc[...] = jnp.zeros_like(acc)
        total = total_of(own_ref, other_refs)
        for i, ref in enumerate(w_refs):
            rows = slice(i * dim, (i + 1) * dim)
            fresh[rows] = (ref[0].astype(F32) + scale * total[rows]).astype(BF16)

    q = stacked(pieces, 0)
    o = stacked(pieces, 1)
    w_gate, w_up, w_down = fresh[:dim], fresh[dim : 2 * dim], fresh[2 * dim :]
    gate = mm(q, w_gate)
    up = mm(q, w_up)
    dhid = mm_nt(o, w_down)
    sig = sigmoid(gate)
    act = gate * sig
    hidden = (act * up).astype(BF16)
    dgate = (dhid * up * (sig * (1.0 + gate * (1.0 - sig)))).astype(BF16)
    dup = (dhid * act).astype(BF16)
    grad = (mm_nt(dgate, w_gate) + mm_nt(dup, w_up)).astype(BF16)
    rows = grads[0].shape[0]
    for j, ref in enumerate(grads):
        ref[...] = grad[j * rows : (j + 1) * rows]
    acc[:dim] += mm_tn(q, dgate)
    acc[dim : 2 * dim] += mm_tn(q, dup)
    acc[2 * dim :] += mm_tn(hidden, o)

    @pl.when(step == pl.num_programs(0) - 1)
    def _():
        sent_ref[...] = acc[...].astype(BF16)


def back_kernel(scale, n_group, n_s, n_other, at_ref, *refs):
    pieces, refs = refs[:n_group], refs[n_group:]
    rate_refs, refs = refs[:n_s], refs[n_s:]
    w_gate, w_up, w_down = (ref[0] for ref in refs[:3])
    own_ref, other_refs = refs[3], refs[4 : 4 + n_other]
    outs, adj, tall = refs[4 + n_other : -2], refs[-2], refs[-1]
    dim = pieces[0].shape[-1]

    @pl.when(pl.program_id(0) == 0)
    def _():
        adj[...] = (scale * total_of(own_ref, other_refs)).astype(BF16)
        fill_rates(at_ref, rate_refs, tall)

    k = stacked(pieces, 0)
    rate = tall_rates(tall, pieces[0].shape[1], dim)
    scaled = (rate * stacked(pieces, 1).astype(F32)).astype(BF16)
    adj_gate, adj_up, adj_down = adj[:dim], adj[dim : 2 * dim], adj[2 * dim :]
    gate = mm(k, w_gate)
    up = mm(k, w_up)
    dhid = mm_nt(scaled, w_down)
    sig = sigmoid(gate)
    act = gate * sig
    rest = 1.0 - sig
    slope = sig * (1.0 + gate * rest)
    curve = sig * rest * (2.0 + gate * (1.0 - 2.0 * sig))
    hidden = (act * up).astype(BF16)
    dgate = (dhid * up * slope).astype(BF16)
    dup = (dhid * act).astype(BF16)
    back_dgate = mm(k, adj_gate)
    back_dup = mm(k, adj_up)
    back_hidden = mm_nt(scaled, adj_down)
    back_scaled = mm(hidden, adj_down)
    back_dhid = (back_dgate * up * slope + back_dup * act).astype(BF16)
    back_gate = (
        back_dgate * dhid * up * curve + (back_dup * dhid + back_hidden * up) * slope
    ).astype(BF16)
    back_upper = (back_dgate * dhid * slope + back_hidden * act).astype(BF16)
    grad_k = mm_nt(dgate, adj_gate) + mm_nt(dup, adj_up)
    grad_k = (grad_k + mm_nt(back_gate, w_gate) + mm_nt(back_upper, w_up)).astype(BF16)
    grad_v = (rate * (back_scaled + mm(back_dhid, w_down))).astype(BF16)
    rows = outs[0].shape[1]
    for j, ref in enumerate(outs):
        ref[0] = grad_k[j * rows : (j + 1) * rows]
        ref[1] = grad_v[j * rows : (j + 1) * rows]


def body(n_t, n_s, n_head, queries, key_tokens, values, out_grad, learn_rates, w_gate, w_up, w_down):
    rows, model = queries.shape
    n_group = n_head * n_s
    dim = model // (n_group * HEADS_HELD)
    held = range(HEADS_HELD)
    hops = [1 << i for i in range(n_t.bit_length() - 1)] if n_t & (n_t - 1) == 0 else None
    tile = min(rows, 128)
    grid = (rows // tile,)
    fine = min(rows, 64)
    steps = (rows // fine,)
    scale = 1.0 / math.sqrt(dim * rows * n_group * n_t)
    place = lax.axis_index("head") * n_s + lax.axis_index("s")
    at = jnp.stack([place, lax.axis_index("t")]).astype(jnp.int32)

    def partners(j):
        pairs = []
        for g in range(n_group):
            ends = [(x % n_s) * n_head + x // n_s for x in (g, g ^ j)]
            pairs.append(tuple(ends))
        return pairs

    params = pltpu.CompilerParams(
        dimension_semantics=("arbitrary",), vmem_limit_bytes=56 * 1024 * 1024
    )
    free = pl.BlockSpec(memory_space=pl.ANY)

    def call(kernel, grid, in_specs, out_specs, out_shape, scratch, *args, after=()):
        n_in = len(args)
        if after:
            inner = kernel

            def kernel(*refs):
                inner(*refs[: n_in + 1], *refs[n_in + 1 + len(after) :])

        return pl.pallas_call(
            kernel,
            out_shape=out_shape,
            grid_spec=pltpu.PrefetchScalarGridSpec(
                num_scalar_prefetch=1,
                grid=grid,
                in_specs=list(in_specs) + [free] * len(after),
                out_specs=out_specs,
                scratch_shapes=scratch,
            ),
            compiler_params=params,
        )(at, *args, *after)

    flat_spec = pl.BlockSpec((tile, model), lambda i, p: (i, 0))
    flat_shape = jax.ShapeDtypeStruct((rows, model), BF16)
    piece_specs = [pl.BlockSpec((2, tile, dim), lambda i, p: (0, i, 0))] * n_group

    def by_head(first, second):
        outs = call(
            functools.partial(by_head_kernel, n_group),
            grid,
            [flat_spec, flat_spec],
            piece_specs * HEADS_HELD,
            [jax.ShapeDtypeStruct((2, rows, dim), BF16)] * (n_group * HEADS_HELD),
            [],
            first,
            second,
        )
        return [outs[a * n_group : (a + 1) * n_group] for a in held]

    def swap(pieces):
        return [pieces[0]] + [
            lax.ppermute(pieces[j], ("s", "head"), partners(j))
            for j in range(1, n_group)
        ]

    def reduce(own, sent):
        if hops is None:
            return own, [lax.psum(sent, "t")]
        others = []
        for i, hop in enumerate(hops):
            if i:
                own = own + others.pop().astype(F32)
                sent = own.astype(BF16)
            others.append(lax.ppermute(sent, "t", [(j, j ^ hop) for j in range(n_t)]))
        return own, others

    sum_spec = pl.BlockSpec((3 * dim, dim), lambda i, p: (0, 0))
    sum_specs = [sum_spec, sum_spec]
    sum_shapes = [
        jax.ShapeDtypeStruct((3 * dim, dim), F32),
        jax.ShapeDtypeStruct((3 * dim, dim), BF16),
    ]

    def rate_specs(a):
        return [pl.BlockSpec((1, n_head, rows), lambda i, p: (a, 0, 0))] * n_s

    fine_specs = [pl.BlockSpec((2, fine, dim), lambda i, p: (0, i, 0))] * n_group
    rate_scratch = pltpu.VMEM((n_group, rows, 128), F32)

    def w_specs(a):
        spec = pl.BlockSpec(
            (1, dim, dim), lambda i, p: (HEADS_HELD * lax.rem(p[0], n_s) + a, 0, 0)
        )
        return [spec] * 3

    weights = (w_gate, w_up, w_down)
    kv = by_head(key_tokens, values)
    kv = [swap(kv[a]) for a in held]
    by_column = learn_rates.T.reshape(n_s, HEADS_HELD, n_head, rows)
    rates = []
    for j in range(n_s):
        piece = by_column[jnp.bitwise_xor(lax.axis_index("s"), j)]
        if j:
            piece = lax.ppermute(piece, "s", [(i, i ^ j) for i in range(n_s)])
        rates.append(piece)
    qo = by_head(queries, out_grad)
    qo = [swap(qo[a]) for a in held]

    def key_forward(a, after=()):
        own, sent = call(
            functools.partial(key_kernel, n_group, n_s),
            steps,
            fine_specs + rate_specs(a) + w_specs(a),
            sum_specs,
            sum_shapes,
            [rate_scratch],
            *kv[a],
            *rates,
            *weights,
            after=after,
        )
        return own, reduce(own, sent)

    def query_side(a, own, others, after=()):
        outs = call(
            functools.partial(query_kernel, scale, n_group, len(others)),
            steps,
            fine_specs + w_specs(a) + [sum_spec] * (1 + len(others)),
            [pl.BlockSpec((fine, dim), lambda i, p: (i, 0))] * n_group + sum_specs,
            [jax.ShapeDtypeStruct((rows, dim), BF16)] * n_group + sum_shapes,
            [pltpu.VMEM((3 * dim, dim), BF16)],
            *qo[a],
            *weights,
            own,
            *others,
            after=after,
        )
        grads, own, sent = outs[:n_group], outs[n_group], outs[n_group + 1]
        return own, reduce(own, sent), swap(grads)

    def key_back(a, own, others, after=()):
        outs = call(
            functools.partial(back_kernel, scale, n_group, n_s, len(others)),
            steps,
            fine_specs + rate_specs(a) + w_specs(a) + [sum_spec] * (1 + len(others)),
            fine_specs,
            [jax.ShapeDtypeStruct((2, rows, dim), BF16)] * n_group,
            [pltpu.VMEM((3 * dim, dim), BF16), rate_scratch],
            *kv[a],
            *rates,
            *weights,
            own,
            *others,
            after=after,
        )
        return outs[0], swap(outs)

    delta, sums, gq, gkv = ([None] * HEADS_HELD for _ in range(4))
    mark = (qo[0][0],)
    for a in held:
        mark, delta[a] = key_forward(a, mark)
        mark = (mark,)
    for a in held:
        mark, sums[a], gq[a] = query_side(a, *delta[a], mark)
        mark = (mark,)
    for a in held:
        mark, gkv[a] = key_back(a, *sums[a], mark)
        mark = (mark,)
    grad_q = call(
        functools.partial(home_kernel, n_group, 1),
        grid,
        [pl.BlockSpec((tile, dim), lambda i, p: (i, 0))] * (HEADS_HELD * n_group),
        [flat_spec],
        [flat_shape],
        [],
        *gq[0],
        *gq[1],
        after=mark,
    )[0]
    grad_k, grad_v = call(
        functools.partial(home_kernel, n_group, 2),
        grid,
        piece_specs * HEADS_HELD,
        [flat_spec] * 2,
        [flat_shape] * 2,
        [],
        *gkv[0],
        *gkv[1],
    )
    return grad_q, grad_k, grad_v


def solution(mesh):
    n_tok, n_head = mesh.shape["tok"], mesh.shape["head"]

    def run(queries, key_tokens, values, out_grad, learn_rates, w_gate, w_up, w_down):
        n_s = w_gate.shape[0] // (n_head * HEADS_HELD)
        n_t = n_tok // n_s
        split = Mesh(mesh.devices.reshape(n_t, n_s, n_head), ("t", "s", "head"))
        tokens = P(("t", "s", "head"), None)
        weights = P("head", None, None)
        return jax.shard_map(
            functools.partial(body, n_t, n_s, n_head),
            mesh=split,
            in_specs=(tokens,) * 4 + (P(("t", "s"), "head"),) + (weights,) * 3,
            out_specs=(tokens,) * 3,
            check_vma=False,
        )(queries, key_tokens, values, out_grad, learn_rates, w_gate, w_up, w_down)


    return run
```
